32 devices in a mesh: vx: 2 (over x), vy: 4 (over y, core), scan: 4 (over z).
Axes of the slice: x: 2, y: 2, z: 4, core: 2. Of those that a mesh axis runs over, the one named last changes fastest.
Arguments:
- volume: bfloat16 [2, 64, 256, 256], P(None, 'vx', 'vy'), may hold values from -6 to 6
- tile_matrix: bfloat16 [4, 2, 8, 1024, 128], P('scan', 'vx', 'vy'), may hold values from -0.09375 to 0.09375
- tile_offset: int32 [4, 2, 8], P('scan', 'vx', 'vy'), may hold values from 0 to 384
- patch_count: int32 [4, 8], P('scan', ('vx', 'vy')), may hold values from 1 to 3, as said below
- scan_position: int32 [4, 8, 3, 2], P('scan', ('vx', 'vy')), may hold values from 0 to 256, as said below
- measured: float32 [4, 8, 3, 256, 256], P('scan', ('vx', 'vy')), may hold values from 0.2 to 5
- illumination: float32 [2, 256, 256], replicated, may hold values from -6 to 6
Outputs:
- change: float32 [2, 64, 256, 256], P(None, 'vx', 'vy', 'scan')
The draws below stay inside these ranges and needn't reach their ends.
Inputs may be any that keep to these rules, and one draw needn't show every extreme that they name: `patch_count`: an owner's slots below its count hold measured patches, the others are unused; at every angle some owner holds 3. `scan_position`: column 0 is a patch's first detector column, 0 to 256; column 1 its first row, 0 to 0.
All inputs are finite; a program needn't handle non-finite values.
Results may differ from the reference program's by a relative error of at most 0.0085.
Values may be sent and summed in bfloat16 or wider, within the bound.
No kernel may reach another device: no remote copies, remote signals or barrier semaphores. Data moves between devices by JAX's collectives and lax.ppermute only.
A program may use at most 64 MiB of HBM per device.

```python
import math
import jax
import jax.numpy as jnp
from jax import lax

TILE = 32
TXD = 1
TYD = 2
NZ = 256
U = 512
TU = 128
PATCH_SIDE = 256
CAP = 3
ITERS = 1
ANGLES = 4
OWNERS = 8
NX = 64
NY = 256
N_VX = 2
N_VY = 4


def draw_patch_count(key, part):
    level_key, owner_key = jax.random.split(key)
    levels = jax.random.randint(level_key, (ANGLES, OWNERS), 0, 8)
    counts = jnp.where(levels == 0, CAP, jnp.where(levels == 1, CAP - 1, 1 + levels % 2))
    chosen = jax.random.randint(owner_key, (ANGLES, 1), 0, OWNERS)
    owners_row = jnp.arange(OWNERS)[None, :]
    return jnp.where(owners_row == chosen, CAP, counts).astype(jnp.int32)


def draw_scan_position(key, part):
    column_key, row_key = jax.random.split(jax.random.fold_in(key, 7))
    columns = jax.random.randint(column_key, (ANGLES, OWNERS, CAP, 1), 0, U - PATCH_SIDE + 1)
    first_rows = jax.random.randint(row_key, (ANGLES, OWNERS, CAP, 1), 0, NZ - PATCH_SIDE + 1)
    return jnp.concatenate([columns, first_rows], axis=3).astype(jnp.int32)


def touch_ends(array, stream_key, least, largest):
    index_at = [jax.random.randint(jax.random.fold_in(stream_key, axis), (), 0, length) for axis, length in enumerate(array.shape)]
    widest = array.shape.index(max(array.shape))
    neighbour = index_at[:widest] + [(index_at[widest] + 1) % array.shape[widest]] + index_at[widest + 1:]
    return array.at[tuple(index_at)].set(least).at[tuple(neighbour)].set(largest)


def steps_of(rng, extent, cuts, low, largest):
    factor_of = 1.0
    for axis_at, parts in cuts:
        heights = jax.random.uniform(jax.random.fold_in(jax.random.fold_in(rng, 6), axis_at), (parts,), jnp.float32, low / len(cuts), largest / len(cuts))
        factor_of = factor_of * jnp.repeat(jnp.exp(heights), extent[axis_at] // parts).reshape((-1,) + (1,) * (len(extent) - 1 - axis_at))
    return factor_of


def bell_draw(rng, dims, deviation, most, shards=(), kind=jnp.bfloat16):
    loudness = steps_of(rng, dims, shards, -0.22, 0.18) if shards else 1.0
    drawn = jax.random.normal(rng, dims, jnp.float32) * deviation * loudness
    return jnp.minimum(jnp.maximum(drawn, -most), most).astype(kind)


def setup_inputs(seed: int = 0) -> dict:
    splits = jax.random.split(jax.random.key(seed), 8)
    volume = bell_draw(splits[0], (2, NX, NY, NZ), 1.0, 6.0, ((1, 2), (2, 4)))
    tile_matrix = bell_draw(splits[1], (ANGLES, TXD * N_VX, TYD * N_VY, TILE * TILE, TU), (TILE * TILE * TXD * TYD * N_VX * N_VY * TU // U) ** -0.5, 0.09375, ((0, 4), (1, 2), (2, 4)))
    tile_offset = touch_ends(jax.random.randint(splits[2], (ANGLES, TXD * N_VX, TYD * N_VY), 0, U - TU + 1), jax.random.fold_in(splits[2], 1), 0, U - TU).astype(jnp.int32)
    patch_count = draw_patch_count(jax.random.fold_in(splits[7], 71), 0)
    scan_position = draw_scan_position(jax.random.fold_in(splits[7], 71), 0)
    measured = jnp.clip(jnp.exp(math.log(5.0) - 3.218876 * jax.random.uniform(splits[5], (ANGLES, OWNERS, CAP, PATCH_SIDE, PATCH_SIDE), jnp.float32) ** steps_of(splits[5], (ANGLES, OWNERS, CAP, PATCH_SIDE, PATCH_SIDE), ((0, 4), (1, 8)), -0.2, 0.2)), 0.2, 5.0)
    illumination = bell_draw(splits[6], (2, PATCH_SIDE, PATCH_SIDE), 1.0, 6.0, (), jnp.float32)
    return dict(volume=volume, tile_matrix=tile_matrix, tile_offset=tile_offset, patch_count=patch_count, scan_position=scan_position, measured=measured, illumination=illumination)


ABSORPTION = 0.2
STEP_LENGTH = 0.003

def dft_tables(length):
    counter = jnp.arange(length, dtype=jnp.int32)
    product = counter[:, None] * counter[None, :] % length
    radians = product.astype(jnp.float32) * (2.0 * math.pi / length)
    scaling = 1.0 / math.sqrt(length)
    return (jnp.cos(radians) * scaling, jnp.sin(radians) * scaling)

def matmul(left, right):
    return jnp.dot(left, right, precision=lax.Precision.HIGHEST)

def patch_misfit(window, illumination, intensity, cosine_table, sine_table):
    amplitude = jnp.exp(-ABSORPTION * window[1])
    trans_re = amplitude * jnp.cos(window[0])
    trans_im = amplitude * jnp.sin(window[0])
    exit_re = illumination[0] * trans_re - illumination[1] * trans_im
    exit_im = illumination[0] * trans_im + illumination[1] * trans_re
    half_re = matmul(cosine_table, exit_re) + matmul(sine_table, exit_im)
    half_im = matmul(cosine_table, exit_im) - matmul(sine_table, exit_re)
    far_re = matmul(half_re, cosine_table) + matmul(half_im, sine_table)
    far_im = matmul(half_im, cosine_table) - matmul(half_re, sine_table)
    residue = far_re * far_re + far_im * far_im - intensity
    return jnp.sum(residue * residue)

def place_patch(summed_total, slope, corner):
    anchor = (jnp.zeros((), jnp.int32), corner[0].astype(jnp.int32), corner[1].astype(jnp.int32))
    before = lax.dynamic_slice(summed_total, anchor, slope.shape)
    return lax.dynamic_update_slice(summed_total, before + slope, anchor)

def volume_tiles(field):
    components, width_x, width_y, depth_cells = field.shape
    blocks = field.reshape(components, width_x // TILE, TILE, width_y // TILE, TILE, depth_cells)
    blocks = blocks.transpose(1, 3, 0, 2, 4, 5)
    return blocks.reshape(-1, components, TILE * TILE, depth_cells)

def tiles_volume(blocks, width_x, width_y):
    components = blocks.shape[1]
    depth_cells = blocks.shape[3]
    shaped = blocks.reshape(width_x // TILE, width_y // TILE, components, TILE, TILE, depth_cells)
    return shaped.transpose(2, 0, 3, 1, 4, 5).reshape(components, width_x, width_y, depth_cells)

def project(current, matrices, offsets):
    blocks = volume_tiles(current)
    flat_mats = matrices.reshape(-1, TILE * TILE, TU)
    flat_offsets = offsets.reshape(-1).astype(jnp.int32)

    def add_tile(summed_total, item):
        weights, offset, block = item
        part_sum = jnp.einsum('ku,ckz->cuz', weights.astype(jnp.float32), block.astype(jnp.float32))
        anchor = (jnp.zeros((), jnp.int32), offset, jnp.zeros((), jnp.int32))
        before = lax.dynamic_slice(summed_total, anchor, part_sum.shape)
        return (lax.dynamic_update_slice(summed_total, before + part_sum, anchor), None)
    start_sum = jnp.zeros((2, U, NZ), jnp.float32)
    summed_total, ignored_value = lax.scan(add_tile, start_sum, (flat_mats, flat_offsets, blocks))
    return summed_total

def misfit_image(projected_field, counts, positions, intensity_values, illumination, cosine_table, sine_table):
    slot_ids = jnp.arange(CAP, dtype=jnp.int32)
    active_mask = (slot_ids[None, :] < counts[:, None]).reshape(-1)
    flattened_positions = positions.reshape(-1, 2).astype(jnp.int32)
    flattened_measurements = intensity_values.reshape(-1, PATCH_SIDE, PATCH_SIDE)
    slope_fn = jax.grad(patch_misfit)

    def slot_to_add(summed_total, item):
        is_live, corner, intensity = item

        def compute(running):
            anchor = (jnp.zeros((), jnp.int32), corner[0], corner[1])
            window = lax.dynamic_slice(projected_field, anchor, (2, PATCH_SIDE, PATCH_SIDE))
            slope = slope_fn(window, illumination, intensity, cosine_table, sine_table)
            return place_patch(running, slope, corner)

        def skipped(running):
            return running
        return (lax.cond(is_live, compute, skipped, summed_total), None)
    summed_total, ignored_value = lax.scan(slot_to_add, jnp.zeros_like(projected_field), (active_mask, flattened_positions, flattened_measurements))
    return summed_total

def backproject(image, matrices, offsets):
    flat_mats = matrices.reshape(-1, TILE * TILE, TU)
    flat_offsets = offsets.reshape(-1).astype(jnp.int32)

    def cut_window(offset):
        anchor = (jnp.zeros((), jnp.int32), offset, jnp.zeros((), jnp.int32))
        return lax.dynamic_slice(image, anchor, (2, TU, NZ))
    windows = jax.vmap(cut_window)(flat_offsets).astype(jnp.bfloat16)
    blocks = jnp.einsum('tku,tcuz->tckz', flat_mats.astype(jnp.float32), windows.astype(jnp.float32))
    return tiles_volume(blocks, NX, NY)

def reference(volume, tile_matrix, tile_offset, patch_count, scan_position, measured, illumination):
    cosine_table, sine_table = dft_tables(PATCH_SIDE)
    iterate = volume.astype(jnp.float32)
    current = volume
    for iteration in range(ITERS):
        slope_sum = jnp.zeros(volume.shape, jnp.float32)
        for angle_index in range(ANGLES):
            projected_field = project(current, tile_matrix[angle_index], tile_offset[angle_index])
            image = misfit_image(projected_field, patch_count[angle_index], scan_position[angle_index], measured[angle_index], illumination, cosine_table, sine_table)
            slope = backproject(image, tile_matrix[angle_index], tile_offset[angle_index])
            rounded = lax.optimization_barrier(slope.astype(jnp.bfloat16))
            slope_sum = slope_sum + rounded.astype(jnp.float32)
        iterate = iterate - STEP_LENGTH * slope_sum
        current = iterate.astype(jnp.bfloat16)
    return iterate - volume.astype(jnp.float32)
```

```python
import functools
import math

import jax
import jax.numpy as jnp
import numpy as np
from jax import lax
from jax.experimental import pallas as pl
from jax.experimental.pallas import tpu as pltpu
from jax.sharding import PartitionSpec as P

TILE = 32
U = 512
ABSORPTION = 0.2
STEP_LENGTH = 0.003
SUBLANES = 8
VMEM_LIMIT = 56 * 1024 * 1024

F32 = jnp.float32
BF16 = jnp.bfloat16
F16 = jnp.float16


def dft_block(length):
    counter = np.arange(length)
    radians = (np.outer(counter, counter) % length) * (2.0 * math.pi / length)
    scaling = 1.0 / math.sqrt(length)
    cosine = np.cos(radians) * scaling
    sine = np.sin(radians) * scaling
    return np.block([[cosine, sine], [-sine, cosine]])


def high_low(table):
    high = table.astype(np.float32).astype(BF16)
    low = (table - high.astype(np.float64)).astype(np.float32).astype(BF16)
    return high, low


def half_pi_parts():
    rest = math.pi / 2
    parts = []
    for bits in (8, 10, 11):
        unit = 2.0 ** (math.floor(math.log2(rest)) - bits + 1)
        part = math.floor(rest / unit) * unit
        parts.append(part)
        rest -= part
    return parts + [rest]


HALF_PI_PARTS = half_pi_parts()


def sine_cosine(angle):
    turns = jnp.round(angle * (2.0 / math.pi))
    rest = angle
    for part in HALF_PI_PARTS:
        rest = rest - turns * part
    quadrant = turns.astype(jnp.int32)
    square = rest * rest
    sine = rest * (
        1.0 + square * (-1 / 6 + square * (1 / 120 + square * (-1 / 5040 + square * (1 / 362880))))
    )
    cosine = 1.0 + square * (
        -0.5 + square * (1 / 24 + square * (-1 / 720 + square * (1 / 40320 - square * (1 / 3628800))))
    )
    swap = (quadrant & 1) == 1
    sine_out = jnp.where(swap, cosine, sine)
    cosine_out = jnp.where(swap, sine, cosine)
    sine_out = jnp.where((quadrant & 2) == 2, -sine_out, sine_out)
    cosine_out = jnp.where(((quadrant + 1) & 2) == 2, -cosine_out, cosine_out)
    return sine_out, cosine_out


def load_rows(ref, lead, start, count):
    base = pl.multiple_of((start // SUBLANES) * SUBLANES, SUBLANES)
    shift = start - base
    block = ref[lead, pl.ds(base, count + SUBLANES), :]
    width = block.shape[-1]
    groups = count // SUBLANES
    turned = pltpu.roll(block.reshape(groups + 1, SUBLANES, width), SUBLANES - shift, 1)
    row = lax.broadcasted_iota(jnp.int32, (groups, SUBLANES, width), 1)
    return jnp.where(row < SUBLANES - shift, turned[:-1], turned[1:]).reshape(count, width)


def add_rows(ref, lead, start, values):
    count, width = values.shape
    groups = count // SUBLANES
    base = pl.multiple_of((start // SUBLANES) * SUBLANES, SUBLANES)
    shift = start - base
    turned = pltpu.roll(values.reshape(groups, SUBLANES, width), shift, 1)
    blank = jnp.zeros((1, SUBLANES, width), values.dtype)
    row = lax.broadcasted_iota(jnp.int32, (groups + 1, SUBLANES, width), 1)
    moved = jnp.where(
        row >= shift,
        jnp.concatenate([turned, blank], 0),
        jnp.concatenate([blank, turned], 0),
    )
    ref[lead, pl.ds(base, count + SUBLANES), :] += moved.reshape(count + SUBLANES, width)


def dot(left, right):
    return jnp.dot(left, right, preferred_element_type=F32)


def split(value):
    high = value.astype(BF16)
    return high, (value - high.astype(F32)).astype(BF16)


class Plan:
    def __init__(self, mesh):
        self.slabs = mesh.shape["scan"]
        self.plane = mesh.shape["vx"] * mesh.shape["vy"]
        bits = self.plane.bit_length() - 1
        self.slab_bits = self.slabs.bit_length() - 1
        assert 1 << bits == self.plane and 1 << self.slab_bits == self.slabs
        groups = [(0, 1)]
        low = 1
        while low < bits:
            size = min(2, bits - low)
            groups.append((low, size))
            low += size
        self.groups = groups
        order = [0]
        for low, size in groups:
            order = [known | (digit << low) for known in order for digit in range(1 << size)]
        self.order = order

    def slab_digit(self, index):
        return (index >> 1) & (self.slabs - 1)

    def chunk_digit(self, index):
        return (index & 1) | ((index >> (1 + self.slab_bits)) << 1)


def plane_send(value, plan, mask):
    pairs = [(index, index ^ mask) for index in range(plan.plane)]
    return lax.ppermute(value, ("vx", "vy"), pairs)


def scatter_stage(keep, sends, plan, group):
    low = group[0]
    total = keep
    for digit, send in sends:
        total = total + plane_send(send, plan, digit << low).astype(F32)
    return total


def split_stage(total, group, dtype):
    parts = total.reshape((1 << group[1], -1) + total.shape[1:])
    return parts[0], [(digit, parts[digit].astype(dtype)) for digit in range(1, 1 << group[1])]


def gather_pieces(piece, plan):
    held = [(0, piece)]
    for low, size in reversed(plan.groups):
        arrived = []
        for digit in range(1, 1 << size):
            arrived += [
                (mask | (digit << low), plane_send(value, plan, digit << low)) for mask, value in held
            ]
        held = held + arrived
    return held


def project_kernel(plan, place_ref, offset_ref, volume_ref, matrix_ref, out_ref, image_ref):
    tiles, _, reach = matrix_ref.shape
    components, _, width_y, depth = volume_ref.shape
    tiles_y = width_y // TILE
    me = place_ref[0]
    image_ref[...] = jnp.zeros_like(image_ref)
    for tile in range(tiles):
        tile_x, tile_y = divmod(tile, tiles_y)
        rows = slice(tile_x * TILE, (tile_x + 1) * TILE)
        columns = slice(tile_y * TILE, (tile_y + 1) * TILE)
        for part in range(components):
            block = volume_ref[part, rows, columns, :].reshape(TILE * TILE, depth)
            cast = lax.dot_general(
                matrix_ref[tile], block, (((0,), (0,)), ((), ())), preferred_element_type=F32
            )
            add_rows(image_ref, part, offset_ref[tile], cast)
    length = out_ref.shape[1]
    per_part = U // length
    for spot, mask in enumerate(plan.order):
        piece = me ^ mask
        start = pl.multiple_of((piece % per_part) * length, SUBLANES)
        out_ref[spot] = image_ref[piece // per_part, pl.ds(start, length), :]


def patch_kernel(
    plan, passes, place_ref, count_ref, corner_ref, *refs
):
    pieces = refs[: plan.plane]
    (measured_ref, illumination_ref, left_high, left_low, right_high, right_low,
     keep_ref, send_ref, field_ref, image_ref) = refs[plan.plane:]
    forward, backward = passes
    me = place_ref[0]
    angle = place_ref[1]
    slots, side, _ = measured_ref.shape
    length = pieces[0].shape[0]
    per_part = U // length
    for (mask, piece_ref) in zip(plan.order, pieces):
        piece = me ^ mask
        start = pl.multiple_of((piece % per_part) * length, SUBLANES)
        field_ref[piece // per_part, pl.ds(start, length), :] = piece_ref[...]
    image_ref[...] = jnp.zeros_like(image_ref)

    def left(high, low, value, count):
        if count == 1:
            return dot(high[...], value.astype(BF16))
        upper, lower = split(value)
        total = dot(high[...], upper) + dot(low[...], upper)
        return total + dot(high[...], lower) if count == 3 else total

    def right(value, high, low, count):
        if count == 1:
            return dot(value.astype(BF16), high[...])
        upper, lower = split(value)
        total = dot(upper, high[...]) + dot(upper, low[...])
        return total + dot(lower, high[...]) if count == 3 else total

    def slot_step(slot, carry):
        start = corner_ref[slot]
        phase = load_rows(field_ref, 0, start, side)
        absorbed = load_rows(field_ref, 1, start, side)
        amplitude = jnp.exp(-ABSORPTION * absorbed)
        sine, cosine = sine_cosine(phase)
        trans_re = amplitude * cosine
        trans_im = amplitude * sine
        exit_re = illumination_ref[0] * trans_re - illumination_ref[1] * trans_im
        exit_im = illumination_ref[0] * trans_im + illumination_ref[1] * trans_re
        stacked = jnp.concatenate([exit_re, exit_im], axis=0)
        half = left(left_high, left_low, stacked, forward)
        half = jnp.concatenate([half[:side], half[side:]], axis=1)
        far = right(half, right_high, right_low, forward)
        far_re = far[:, :side]
        far_im = far[:, side:]
        residue = 4.0 * (far_re * far_re + far_im * far_im - measured_ref[slot])
        slope = jnp.concatenate([residue * far_re, residue * far_im], axis=1)
        slope = right(slope, left_high, left_low, backward)
        slope = jnp.concatenate([slope[:, :side], slope[:, side:]], axis=0)
        slope = left(right_high, right_low, slope, backward)
        slope_re = slope[:side]
        slope_im = slope[side:]
        add_rows(image_ref, 0, start, exit_re * slope_im - exit_im * slope_re)
        add_rows(image_ref, 1, start, -ABSORPTION * (exit_re * slope_re + exit_im * slope_im))
        return carry

    lax.fori_loop(0, count_ref[0], slot_step, 0)

    lanes = keep_ref.shape[-1]
    half_lanes = lanes // 2
    chunk_rows = keep_ref.shape[1]
    kept = keep_ref.shape[0]
    column = lax.broadcasted_iota(jnp.int32, (chunk_rows, lanes), 1)
    for spot, mask in enumerate(plan.order):
        target = me ^ mask
        slab = angle ^ plan.slab_digit(target)
        rows = pl.ds(pl.multiple_of(plan.chunk_digit(target) * chunk_rows, SUBLANES), chunk_rows)
        across = pl.ds(pl.multiple_of((slab // 2) * lanes, 128), lanes)
        odd = (slab % 2) * half_lanes
        first = pltpu.roll(image_ref[0, rows, across], odd, 1)
        second = pltpu.roll(image_ref[1, rows, across], half_lanes - odd, 1)
        packed = jnp.where(column < half_lanes, first, second)
        if spot < kept:
            keep_ref[spot] = packed
        else:
            send_ref[spot - kept] = packed.astype(BF16)


def back_kernel(plan, place_ref, offset_ref, *refs):
    pieces = refs[: plan.plane]
    own_ref, near_ref, inner_two, inner_three, outer_two, outer_three, out_ref, window_ref = refs[
        plan.plane:
    ]
    me = place_ref[0]
    angle = place_ref[1]
    inside = (angle > 0) & (angle < plan.slabs - 1)
    tiles, cells, reach = own_ref.shape
    tiles_y = out_ref.shape[2] // TILE
    rows, lanes = pieces[0].shape
    depth = lanes // 2
    for mask, piece_ref in zip(plan.order, pieces):
        source = me ^ mask
        start = pl.multiple_of(plan.chunk_digit(source) * rows, SUBLANES)
        window_ref[plan.slab_digit(source), pl.ds(start, rows), :] = piece_ref[...].astype(F32)
    for tile in range(tiles):
        two = jnp.where(inside, inner_two[tile], outer_two[tile])
        three = jnp.where(inside, inner_three[tile], outer_three[tile])
        weights = jnp.concatenate([own_ref[tile], near_ref[tile], two, three], axis=1)
        windows = jnp.concatenate(
            [
                load_rows(window_ref, other, offset_ref[other, tile], reach).astype(BF16)
                for other in range(plan.slabs)
            ],
            axis=0,
        )
        block = dot(weights, windows) * (-STEP_LENGTH)
        tile_x, tile_y = divmod(tile, tiles_y)
        at_x = slice(tile_x * TILE, (tile_x + 1) * TILE)
        at_y = slice(tile_y * TILE, (tile_y + 1) * TILE)
        out_ref[0, at_x, at_y, :] = block[:, :depth].reshape(TILE, TILE, depth)
        out_ref[1, at_x, at_y, :] = block[:, depth:].reshape(TILE, TILE, depth)


def vmem(count):
    return [pl.BlockSpec(memory_space=pltpu.VMEM)] * count


def smem(count):
    return [pl.BlockSpec(memory_space=pltpu.SMEM)] * count


def kernel_call(body, out_shape, scalars, arrays, scratch):
    outs = len(out_shape) if isinstance(out_shape, list) else 1
    return pl.pallas_call(
        body,
        out_shape=out_shape,
        in_specs=smem(len(scalars)) + vmem(len(arrays)),
        out_specs=vmem(outs) if outs > 1 else vmem(1)[0],
        scratch_shapes=scratch,
        compiler_params=pltpu.CompilerParams(vmem_limit_bytes=VMEM_LIMIT),
    )(*scalars, *arrays)


def scan_send(value, pairs):
    return lax.ppermute(value, "scan", pairs)


def gather_matrices(matrices, slabs):
    swap = [(index, index ^ 1) for index in range(slabs)]
    middle = [(1, 2), (2, 1)]
    outward = [(1, 0), (2, 3)]
    near = scan_send(matrices, swap)
    inner_three = scan_send(matrices, middle)
    inner_two = scan_send(near, middle)
    outer_two = scan_send(inner_three, outward)
    outer_three = scan_send(inner_two, outward)
    return near, inner_two, inner_three, outer_two, outer_three


def per_device(
    plan, axis_names, volume, tile_matrix, tile_offset, patch_count, scan_position, measured, illumination
):
    slabs = plan.slabs
    assert slabs == 4
    reach = tile_matrix.shape[-1]
    matrices = tile_matrix[0].reshape(-1, TILE * TILE, reach)
    offsets = tile_offset[0].reshape(-1)
    side = measured.shape[-1]
    depth = volume.shape[-1]
    me = lax.axis_index(("vx", "vy"))
    angle = lax.axis_index("scan")
    place = jnp.stack([me, angle]).astype(jnp.int32)
    near, inner_two, inner_three, outer_two, outer_three = gather_matrices(matrices, slabs)
    all_offsets = jnp.stack(
        [offsets]
        + [
            scan_send(offsets, [(index, index ^ mask) for index in range(slabs)])
            for mask in range(1, slabs)
        ]
    )

    length = 2 * U // plan.plane
    projected = kernel_call(
        functools.partial(project_kernel, plan),
        jax.ShapeDtypeStruct((plan.plane, length, depth), F32),
        [place, offsets],
        [volume, matrices],
        [pltpu.VMEM((2, U + SUBLANES, depth), F32)],
    )
    for group in plan.groups:
        keep, sends = split_stage(projected, group, F16)
        projected = scatter_stage(keep, sends, plan, group)
    pieces = dict(gather_pieces(projected[0].astype(F16), plan))
    pieces = [pieces[mask].astype(F32) for mask in plan.order]

    table = dft_block(side)
    tables = [jnp.asarray(item) for item in high_low(table) + high_low(table.T)]
    chunk_rows = U * slabs // plan.plane
    lanes = 2 * depth // slabs
    halves = plan.plane // 2
    keep, send = kernel_call(
        functools.partial(patch_kernel, plan, (3, 1)),
        [
            jax.ShapeDtypeStruct((halves, chunk_rows, lanes), F32),
            jax.ShapeDtypeStruct((halves, chunk_rows, lanes), BF16),
        ],
        [place, patch_count[0], scan_position[0, 0, :, 0]],
        pieces + [measured[0, 0], illumination] + tables,
        [pltpu.VMEM((2, U + SUBLANES, depth), F32)] * 2,
    )
    total = scatter_stage(keep, [(1, send)], plan, plan.groups[0])
    for group in plan.groups[1:]:
        keep, sends = split_stage(total, group, BF16)
        total = scatter_stage(keep, sends, plan, group)
    route = [
        (index * slabs + at, index * slabs + (at ^ plan.slab_digit(index)))
        for index in range(plan.plane)
        for at in range(slabs)
    ]
    moved = lax.ppermute(total[0].astype(BF16), axis_names, route)
    windows = dict(gather_pieces(moved, plan))
    return kernel_call(
        functools.partial(back_kernel, plan),
        jax.ShapeDtypeStruct(volume.shape[:3] + (depth // slabs,), F32),
        [place, all_offsets],
        [windows[mask] for mask in plan.order]
        + [matrices, near, inner_two, inner_three, outer_two, outer_three],
        [pltpu.VMEM((slabs, U + SUBLANES, lanes), F32)],
    )


def solution(mesh):
    in_specs = (
        P(None, "vx", "vy", None),
        P("scan", "vx", "vy", None, None),
        P("scan", "vx", "vy"),
        P("scan", ("vx", "vy")),
        P("scan", ("vx", "vy"), None, None),
        P("scan", ("vx", "vy"), None, None, None),
        P(),
    )
    out_specs = P(None, "vx", "vy", "scan")
    body = functools.partial(per_device, Plan(mesh), tuple(mesh.axis_names))
    return jax.shard_map(body, mesh=mesh, in_specs=in_specs, out_specs=out_specs, check_vma=False)
```
